32 devices in a mesh: tm: 16 (over z, y, x), rows: 2 (over core).
Axes of the slice: x: 2, y: 2, z: 4, core: 2. Of those that a mesh axis runs over, the one named last changes fastest.
Arguments:
- latents: bfloat16 [64, 8, 5120], P('tm', 'rows'), may hold values from -25 to 25
- cotangent: bfloat16 [64, 8, 5120], P('tm', 'rows'), may hold values from -6 to 6
- kernel_one: bfloat16 [3, 3, 3, 64, 64], replicated, may hold values from -0.15625 to 0.15625
- kernel_two: bfloat16 [3, 3, 3, 64, 64], replicated, may hold values from -0.15625 to 0.15625
- gain_one: float32 [64], replicated, may hold values from 0.5 to 1.5
- offset_one: float32 [64], replicated, may hold values from -3 to 3
- gain_two: float32 [64], replicated, may hold values from 0.5 to 1.5
- offset_two: float32 [64], replicated, may hold values from -3 to 3
- clip_id: int32 [64], P('tm'), may hold values from 0 to 7, never falling along the last dimension, each value on 1 to 16 neighbouring positions
Outputs:
- output: bfloat16 [64, 8, 5120], P('tm', 'rows')
- grad_latent: bfloat16 [64, 8, 5120], P('tm', 'rows')
- grad_kernel_one: float32 [3, 3, 3, 64, 64], replicated
- grad_kernel_two: float32 [3, 3, 3, 64, 64], replicated
The draws below stay inside these ranges and needn't reach their ends.
Inputs may be any that keep to these rules, and one draw needn't show every extreme that they name: `clip_id`: clip numbers never fall along the frames; each clip number 0 to 7 names 1 to 16 consecutive frames, and one clip has exactly 16.
All inputs are finite; a program needn't handle non-finite values.
Results may differ from the reference program's by a relative error of at most 0.0085.
Values may be sent and summed in bfloat16 or wider, within the bound.
A program may use at most 128 MiB of HBM per device.

```python
import math
import jax
import jax.numpy as jnp
import numpy as np
from jax import lax

C = 64
GROUPS = 32
W = 80
FRAMES = 64
H = 8
CLIPS = 8
MOST = 16


def draw_latents(key, part):
    key_base, key_rough, key_offset = jax.random.split(key, 3)
    ramp = 1.0 + 2.0 * jnp.arange(FRAMES, dtype=jnp.float32) / FRAMES
    rough = jnp.exp(jax.random.uniform(key_rough, (FRAMES, H, 1), jnp.float32, math.log(0.5), math.log(2.0)))
    offset = jax.random.uniform(key_offset, (C,), jnp.float32, -1.0, 1.0)
    offset_full = jnp.tile(offset, W)
    base = jnp.clip(jax.random.normal(key_base, (FRAMES, H, W * C), jnp.float32), -4.0, 4.0)
    values = base * rough * ramp[:, None, None] + offset_full[None, None, :]
    return values.astype(jnp.bfloat16)


def level_of(own_key, shape, cuts, least, high):
    def one(position, parts):
        steps = jax.random.uniform(jax.random.fold_in(jax.random.fold_in(own_key, 6), position), (parts,), jnp.float32, least / len(cuts), high / len(cuts))
        return jnp.repeat(jnp.exp(steps), shape[position] // parts).reshape((-1,) + (1,) * (len(shape) - position - 1))

    loudness = one(*cuts[0])
    for cut in cuts[1:]:
        loudness = loudness * one(*cut)
    return loudness


def profile(count, total, limit, skew):
    loads = [(1 << 20) // math.isqrt(grade ** skew) + 1 for grade in range(2, count + 1)]
    rest, given = total - limit - (count - 1), [1] * (count - 1)
    while rest > 0:
        free = [i for i in range(count - 1) if given[i] < limit]
        whole, budget = sum([loads[i] for i in free]), rest
        for i in free:
            addition = min(limit - given[i], max(1, budget * loads[i] // whole), rest)
            given[i] = given[i] + addition
            rest = rest - addition
    return np.array([limit] + given)


def ragged(stream_key, number_of, total, most, skew):
    if number_of == 2:
        one = jax.random.randint(stream_key, (), max(1, total - most), min(most, total - 1) + 1)
        return jnp.stack([one, total - one])
    sizes = jnp.asarray(profile(number_of, total, most, skew), jnp.int32)
    couples = (number_of - 1) // 2
    donor, receiver = sizes[1:1 + 2 * couples:2], sizes[2:2 + 2 * couples:2]
    slack = jnp.minimum(donor - 1, most - receiver)
    passed = jax.random.randint(jax.random.fold_in(stream_key, 1), (couples,), 0, 1 << 20) % (slack + 1)
    sizes = sizes.at[1:1 + 2 * couples:2].set(donor - passed).at[2:2 + 2 * couples:2].set(receiver + passed)
    return sizes[jax.random.permutation(jax.random.fold_in(stream_key, 2), number_of)]


def normal_values(own_key, shape, deviation, bound, shards=(), held_as=jnp.bfloat16):
    array = jax.random.normal(own_key, shape, jnp.float32) * deviation
    if len(shards) > 0:
        array = level_of(own_key, shape, shards, -0.22, 0.18) * array
    return jnp.clip(array, min=-bound, max=bound).astype(held_as)


def setup_inputs(seed: int = 0) -> dict:
    seeds = jax.random.split(jax.random.key(seed), 10)
    latents = draw_latents(jax.random.fold_in(seeds[9], 71), 0)
    cotangent = normal_values(seeds[1], (FRAMES, H, W * C), 1.0, 6.0, ((0, 16), (1, 2)))
    kernel_one = normal_values(seeds[2], (3, 3, 3, C, C), (27 * C) ** -0.5, 0.15625)
    kernel_two = normal_values(seeds[3], (3, 3, 3, C, C), (27 * C) ** -0.5, 0.15625)
    gain_one = jnp.clip(jax.random.uniform(seeds[4], (C,), jnp.float32, 0.5, 1.5), 0.5, 1.5)
    offset_one = normal_values(seeds[5], (C,), 0.5, 3.0, (), jnp.float32)
    gain_two = jnp.clip(jax.random.uniform(seeds[6], (C,), jnp.float32, 0.5, 1.5), 0.5, 1.5)
    offset_two = normal_values(seeds[7], (C,), 0.5, 3.0, (), jnp.float32)
    clip_id = jnp.searchsorted(jnp.cumsum(ragged(seeds[8], CLIPS, FRAMES, MOST, 1)), jnp.arange(FRAMES), side="right").astype(jnp.int32)
    return {"latents": latents, "cotangent": cotangent, "kernel_one": kernel_one, "kernel_two": kernel_two, "gain_one": gain_one, "offset_one": offset_one, "gain_two": gain_two, "offset_two": offset_two, "clip_id": clip_id}


EPSILON = 1e-06

def delay(field, lag):
    if lag == 0:
        return field
    return jnp.concatenate([jnp.zeros_like(field[:lag]), field[:-lag]], axis=0)

def advance(field, lag):
    if lag == 0:
        return field
    return jnp.concatenate([field[lag:], jnp.zeros_like(field[:lag])], axis=0)

def lag_masks(clip_id):
    tags = clip_id + 1
    return [(delay(tags, lag) == tags).astype(jnp.float32) for lag in range(3)]

def lead_masks(clip_id):
    tags = clip_id + 1
    return [(advance(tags, lag) == tags).astype(jnp.float32) for lag in range(3)]

def pad_space(field):
    return jnp.pad(field, ((0, 0), (1, 1), (1, 1), (0, 0)))

def causal_conv(field, kernel, masks):
    n_rows, n_cols = (field.shape[1], field.shape[2])
    result = jnp.zeros(field.shape[:3] + (kernel.shape[4],), jnp.float32)
    for lag in range(3):
        shifted = pad_space(delay(field, lag) * masks[lag][:, None, None, None].astype(jnp.bfloat16))
        for row_tap in range(3):
            for col_tap in range(3):
                window = shifted[:, row_tap:row_tap + n_rows, col_tap:col_tap + n_cols].astype(jnp.float32)
                result = result + jnp.einsum('fhwc,cd->fhwd', window, kernel[lag, row_tap, col_tap].astype(jnp.float32), precision=lax.Precision.HIGHEST)
    return result

def conv_transpose(grad, kernel, leads):
    n_rows, n_cols = (grad.shape[1], grad.shape[2])
    result = jnp.zeros(grad.shape[:3] + (kernel.shape[3],), jnp.float32)
    for lag in range(3):
        shifted = pad_space(advance(grad, lag) * leads[lag][:, None, None, None].astype(jnp.bfloat16))
        for row_tap in range(3):
            for col_tap in range(3):
                window = shifted[:, 2 - row_tap:2 - row_tap + n_rows, 2 - col_tap:2 - col_tap + n_cols].astype(jnp.float32)
                result = result + jnp.einsum('fhwd,cd->fhwc', window, kernel[lag, row_tap, col_tap].astype(jnp.float32), precision=lax.Precision.HIGHEST)
    return result

def kernel_grad(field, grad, masks):
    n_rows, n_cols = (field.shape[1], field.shape[2])
    grad_wide = grad.astype(jnp.float32)
    lag_list = []
    for lag in range(3):
        shifted = pad_space(delay(field, lag) * masks[lag][:, None, None, None].astype(jnp.bfloat16))
        row_list = []
        for row_tap in range(3):
            col_list = []
            for col_tap in range(3):
                window = shifted[:, row_tap:row_tap + n_rows, col_tap:col_tap + n_cols].astype(jnp.float32)
                col_list.append(jnp.einsum('fhwc,fhwd->cd', window, grad_wide, precision=lax.Precision.HIGHEST))
            row_list.append(jnp.stack(col_list))
        lag_list.append(jnp.stack(row_list))
    return jnp.stack(lag_list)

def clip_sum(per_frame, clip_id):
    table = jax.ops.segment_sum(per_frame, clip_id, num_segments=CLIPS)
    return table[clip_id]

def norm_forward(field, gain, offset, clip_id):
    n_frames, n_rows, n_cols, channels = field.shape
    per_group = channels // GROUPS
    grouped = field.reshape(n_frames, n_rows * n_cols, GROUPS, per_group)
    first = lax.optimization_barrier(jnp.sum(grouped, axis=(1, 3)))
    second = lax.optimization_barrier(jnp.sum(grouped * grouped, axis=(1, 3)))
    cells_count = clip_sum(jnp.ones((n_frames, 1), jnp.float32), clip_id) * float(n_rows * n_cols * per_group)
    mean_val = clip_sum(first, clip_id) / cells_count
    square_mean = clip_sum(second, clip_id) / cells_count
    inv_std = lax.rsqrt(square_mean - mean_val * mean_val + EPSILON)
    normed = (grouped - mean_val[:, None, :, None]) * inv_std[:, None, :, None]
    z_value = normed * gain.reshape(1, 1, GROUPS, per_group) + offset.reshape(1, 1, GROUPS, per_group)
    return (normed, z_value, inv_std, cells_count)

def norm_backward(grad, normed, z_value, inv_std, cells_count, gain, clip_id):
    per_group = normed.shape[3]
    grouped_grad = grad.reshape(normed.shape)
    sigmoid_z = jax.nn.sigmoid(z_value)
    grad_norm = grouped_grad * sigmoid_z * (1.0 + z_value * (1.0 - sigmoid_z)) * gain.reshape(1, 1, GROUPS, per_group)
    p_term = clip_sum(lax.optimization_barrier(jnp.sum(grad_norm, axis=(1, 3))), clip_id) / cells_count
    q_term = clip_sum(lax.optimization_barrier(jnp.sum(grad_norm * normed, axis=(1, 3))), clip_id) / cells_count
    result = inv_std[:, None, :, None] * (grad_norm - p_term[:, None, :, None] - normed * q_term[:, None, :, None])
    return result.reshape(grad.shape)

def reference(latents, cotangent, kernel_one, kernel_two, gain_one, offset_one, gain_two, offset_two, clip_id):
    shape_four = (FRAMES, H, W, C)
    masks = lag_masks(clip_id)
    leads = lead_masks(clip_id)
    field = latents.reshape(shape_four).astype(jnp.float32)
    normed_one, z_one, inv_one, cells_count = norm_forward(field, gain_one, offset_one, clip_id)
    act_one = jax.nn.silu(z_one).astype(jnp.bfloat16).reshape(shape_four)
    hidden = causal_conv(act_one, kernel_one, masks).astype(jnp.bfloat16)
    normed_two, z_two, inv_two, count_again = norm_forward(hidden.astype(jnp.float32), gain_two, offset_two, clip_id)
    act_two = jax.nn.silu(z_two).astype(jnp.bfloat16).reshape(shape_four)
    output = (field + causal_conv(act_two, kernel_two, masks)).astype(jnp.bfloat16).reshape(latents.shape)
    grad_out = cotangent.reshape(shape_four)
    grad_two = kernel_grad(act_two, grad_out, masks)
    back_two = conv_transpose(grad_out, kernel_two, leads)
    grad_hidden = norm_backward(back_two, normed_two, z_two, inv_two, count_again, gain_two, clip_id).astype(jnp.bfloat16)
    grad_one = kernel_grad(act_one, grad_hidden, masks)
    back_one = conv_transpose(grad_hidden, kernel_one, leads)
    branch = norm_backward(back_one, normed_one, z_one, inv_one, cells_count, gain_one, clip_id)
    grad_latent = (grad_out.astype(jnp.float32) + branch).astype(jnp.bfloat16).reshape(latents.shape)
    return (output, grad_latent, grad_one, grad_two)
```

```python
import functools
import jax
import jax.numpy as jnp
from jax import lax
from jax.experimental import pallas as pl
from jax.experimental.pallas import tpu as pltpu
from jax.sharding import PartitionSpec as P

EPSILON = 1e-06
REACH = 4
SLOTS = 2 * (2 * REACH + 1)
OWN = 2 * REACH
PAIRS = 48
PIECES = 27
ALL = 32
MESH = pl.DeviceIdType.MESH
F32 = jnp.float32
BF16 = jnp.bfloat16


def kernel(
    n_tm, n_cols, lat_ref, cot_ref, ids_ref, w1_ref, w1t_ref, w2_ref, w2t_ref, vec_ref,
    out_ref, gl_ref, g1_ref, g2_ref,
    lat, cot, hid, err, stats, win_one, win_two, win_cot, win_back,
    stat_send, stat_recv, halo_send, halo_recv, *shared,
):
    direct = len(shared) > 0
    me = lax.axis_index("tm")
    core = lax.axis_index("rows")
    cells = 16 * PAIRS

    def within(d):
        if d == 0:
            return None
        return me + d < n_tm if d > 0 else me + d >= 0

    def guarded(cond, fn):
        if cond is None:
            fn()
        else:
            pl.when(cond)(fn)

    peers = [
        (d, o) for d in range(-REACH, REACH + 1) for o in range(2) if (d, o) != (0, 0)
    ]

    def device(d, o):
        return (me + d, core if o == 0 else 1 - core)

    def stat_copy(turn, d, o):
        slot = (REACH - d) * 2 + o
        return pltpu.make_async_remote_copy(
            src_ref=stats.at[turn, OWN],
            dst_ref=stats.at[turn, slot],
            send_sem=stat_send.at[turn, slot],
            recv_sem=stat_recv.at[turn, slot],
            device_id=device(d, o),
            device_id_type=MESH,
        )

    def send_stats(turn):
        for d, o in peers:
            guarded(within(d), lambda d=d, o=o: stat_copy(turn, d, o).start())

    def recv_stats(turn):
        for d, o in peers:
            guarded(within(-d), lambda d=d, o=o: stat_copy(turn, d, o).wait_recv())

    row_from = 4 - 3 * core
    row_to = 5 * core
    spans = {"past": (1, 4, 0, 2), "here": (0, 2, 2, 4), "next": (-1, 2, 6, 2)}

    def halo_copy(index, buf, kind, o):
        d, start, to, size = spans[kind]
        if o == 0:
            src = buf.at[pl.ds(start, size), pl.ds(1, 4)]
            dst = buf.at[pl.ds(to, size), pl.ds(1, 4)]
        else:
            src = buf.at[pl.ds(start, size), pl.ds(row_from, 1)]
            dst = buf.at[pl.ds(to, size), pl.ds(row_to, 1)]
        return pltpu.make_async_remote_copy(
            src_ref=src,
            dst_ref=dst,
            send_sem=halo_send.at[index],
            recv_sem=halo_recv.at[index],
            device_id=device(d, o),
            device_id_type=MESH,
        )

    halos = {
        "lat": [(0, lat, "past", 0), (1, lat, "past", 1), (2, lat, "here", 1)],
        "cot": [(3, cot, "next", 0), (4, cot, "next", 1), (5, cot, "here", 1)],
        "err": [(6, err, "next", 0), (7, err, "next", 1), (8, err, "here", 1)],
        "hid": [
            (9, hid, "past", 0), (10, hid, "past", 1), (11, hid, "here", 1),
            (12, hid, "next", 0), (13, hid, "next", 1),
        ],
    }

    def send_halo(name):
        for item in halos[name]:
            guarded(within(spans[item[2]][0]), lambda item=item: halo_copy(*item).start())

    def recv_halo(name):
        for item in halos[name]:
            guarded(
                within(-spans[item[2]][0]), lambda item=item: halo_copy(*item).wait_recv()
            )

    rank = 2 * me + core

    def around(step):
        target = (rank + step) % ALL
        return (target // 2, target % 2)

    def scatter_copy(which, step):
        parts, landing, sums, send, recv = shared[5 * which : 5 * which + 5]
        return pltpu.make_async_remote_copy(
            src_ref=parts.at[(rank + step) % ALL],
            dst_ref=landing.at[step],
            send_sem=send.at[0, step],
            recv_sem=recv.at[0, step],
            device_id=around(step),
            device_id_type=MESH,
        )

    def gather_copy(which, step):
        parts, landing, sums, send, recv = shared[5 * which : 5 * which + 5]
        return pltpu.make_async_remote_copy(
            src_ref=sums.at[rank],
            dst_ref=sums.at[rank],
            send_sem=send.at[1, step],
            recv_sem=recv.at[1, step],
            device_id=around(step),
            device_id_type=MESH,
        )

    owner = rank < PIECES

    def scatter(which):
        for step in range(1, ALL):
            pl.when((rank + step) % ALL < PIECES)(
                lambda step=step: scatter_copy(which, step).start()
            )

    def gather(which):
        parts, landing, sums, send, recv = shared[5 * which : 5 * which + 5]

        @pl.when(owner)
        def _():
            total = parts[rank].astype(F32)
            for step in range(1, ALL):
                scatter_copy(which, step).wait_recv()
            for step in range(1, ALL):
                total = total + landing[step].astype(F32)
            sums[rank] = total.astype(BF16)
            for step in range(1, ALL):
                gather_copy(which, step).start()

    def finish(which, out):
        sums = shared[5 * which + 2]
        for step in range(1, ALL):
            pl.when((rank - step + ALL) % ALL < PIECES)(
                lambda step=step: gather_copy(which, step).wait_recv()
            )
        out[...] = sums[0:PIECES].astype(F32)

    def settle(which):
        for step in range(1, ALL):
            pl.when((rank + step) % ALL < PIECES)(
                lambda step=step: scatter_copy(which, step).wait_send()
            )
            pl.when(owner)(lambda step=step: gather_copy(which, step).wait_send())

    lane = lax.broadcasted_iota(jnp.int32, (1, 128), 1)
    low = lane < 64
    even = lane % 2 == 0

    def grouped(total):
        total = total + pltpu.roll(total, 64, 1)
        return total + jnp.where(even, pltpu.roll(total, 127, 1), pltpu.roll(total, 1, 1))

    def frame_sums(first, second):
        rows = [jnp.sum(v.reshape(4, 4 * PAIRS, 128), axis=1) for v in (first, second)]
        pad = jnp.zeros((4, 128), F32)
        return jnp.concatenate([rows[0], pad]), jnp.concatenate([rows[1], pad])

    def put_stats(turn, first, second):
        a, b = frame_sums(first, second)
        stats[turn, OWN, 0:8] = a
        stats[turn, OWN, 8:16] = b

    for buf in (lat, cot, hid, err):
        buf[...] = jnp.zeros_like(buf)
    stats[...] = jnp.zeros_like(stats)
    lat[2:6, 1:5] = lat_ref[...]
    cot[2:6, 1:5] = cot_ref[...]
    mine = lat_ref[...].astype(F32)
    put_stats(0, mine, mine * mine)
    stats[0, OWN, 16:24] = ids_ref[...]

    barrier = pltpu.get_barrier_semaphore()

    def greet(target):
        pl.semaphore_signal(barrier, inc=1, device_id=target, device_id_type=MESH)

    if direct:
        for step in range(1, ALL):
            greet(around(step))
        pl.semaphore_wait(barrier, ALL - 1)
    else:
        for d, o in peers:
            guarded(within(d), lambda d=d, o=o: greet(device(d, o)))
        reached = jnp.minimum(me, REACH) + jnp.minimum(n_tm - 1 - me, REACH)
        pl.semaphore_wait(barrier, 2 * reached + 1)

    send_stats(0)
    send_halo("cot")
    send_halo("lat")

    g_one, b_one, g_two, b_two = (vec_ref[i : i + 1] for i in range(4))

    pair = lax.broadcasted_iota(jnp.int32, (6, PAIRS, 128), 1)
    image_row = lax.broadcasted_iota(jnp.int32, (6, PAIRS, 128), 0) + 4 * core
    inside = ((pair < n_cols // 2) & (image_row >= 1) & (image_row <= 8)).reshape(
        1, 6, PAIRS, 128
    )
    in_pair = lax.broadcasted_iota(jnp.int32, (1, 1, PAIRS, 128), 2) < n_cols // 2

    def windows(win, field):
        rows = 36 * PAIRS
        cur = field.reshape(rows, 128)
        side = jnp.where(low, pltpu.roll(cur, rows - 1, 0), pltpu.roll(cur, 1, 0))
        win[:, :, :, 0:128] = cur.reshape(6, 6, PAIRS, 128).astype(BF16)
        win[:, :, :, 128:256] = side.reshape(6, 6, PAIRS, 128).astype(BF16)

    def conv(win, weight, first, masks):
        total = None
        for lag in range(3):
            frame = 2 - lag if first else lag
            part = None
            for tap in range(3):
                patch = win[frame : frame + 4, tap : tap + 4].reshape(cells, 256)
                term = jnp.dot(
                    patch, weight[3 * lag + tap], preferred_element_type=F32
                )
                part = term if part is None else part + term
            part = part.reshape(4, 4, PAIRS, 128)
            if lag > 0:
                part = jnp.where(masks[lag], part, 0.0)
            total = part if total is None else total + part
        return jnp.where(in_pair, total, 0.0)

    def kernel_grad(win, grad, masks, out):
        for lag in range(3):
            kept = grad if lag == 0 else jnp.where(masks[lag], grad, 0.0)
            turned = kept.reshape(cells, 128).T.astype(BF16)
            for tap in range(3):
                patch = win[2 - lag : 6 - lag, tap : tap + 4].reshape(cells, 256)
                prod = jnp.dot(turned, patch, preferred_element_type=F32)
                a_lo, a_hi = prod[0:64, 0:128], prod[0:64, 128:256]
                b_lo, b_hi = prod[64:128, 0:128], prod[64:128, 128:256]
                later = a_lo + pltpu.roll(jnp.where(low, b_hi, b_lo), 64, 1)
                early = a_hi + pltpu.roll(b_lo, 64, 1)
                packed = jnp.where(low, pltpu.roll(early[0:32], 64, 1), early[32:64])
                index = 3 * (3 * lag + tap)
                out[index] = later[0:32].astype(out.dtype)
                out[index + 1] = later[32:64].astype(out.dtype)
                out[index + 2] = packed.astype(out.dtype)

    recv_stats(0)
    all_ids = stats[0, :, 16:24].reshape(SLOTS * 8, 128)
    before, own_ids, after = (
        stats[0, OWN - 2, 16:24], stats[0, OWN, 16:24], stats[0, OWN + 2, 16:24]
    )
    ids = [before[2:3], before[3:4]] + [own_ids[f : f + 1] for f in range(4)]
    ids = ids + [after[0:1], after[1:2]]
    match = [(all_ids == i).astype(F32) for i in ids]
    per_slot = float(4 * n_cols * 2)
    count = jnp.concatenate([jnp.sum(m, axis=0, keepdims=True) for m in match])
    count = jnp.maximum(count, 1.0) * per_slot

    def totals(turn):
        both = []
        for part in range(2):
            table = stats[turn, :, 8 * part : 8 * part + 8].reshape(SLOTS * 8, 128)
            rows = [jnp.sum(m * table, axis=0, keepdims=True) for m in match]
            both.append(grouped(jnp.concatenate(rows)) / count)
        return both

    def per_frame(rows, lo, hi):
        return rows[lo:hi].reshape(hi - lo, 1, 1, 128)

    def same(lag, direction):
        rows = [
            jnp.broadcast_to(
                (ids[2 + f] == ids[2 + f + direction * lag]).astype(F32).reshape(1, 1, 1, 128),
                (1, 1, 1, 128),
            )
            for f in range(4)
        ]
        return jnp.concatenate(rows, axis=0) > 0.5

    lags = [None, same(1, -1), same(2, -1)]
    leads = [None, same(1, 1), same(2, 1)]

    recv_halo("cot")
    windows(win_cot, cot[2:8].astype(F32))
    back_two = conv(win_cot, w2t_ref, False, leads)
    err[2:6, 1:5] = back_two
    send_halo("err")

    def moments(turn):
        mean, square = totals(turn)
        return mean, lax.rsqrt(jnp.maximum(square - mean * mean, 0.0) + EPSILON)

    mean_one, rstd_one = moments(0)
    recv_halo("lat")
    normed = (lat[0:6].astype(F32) - per_frame(mean_one, 0, 6)) * per_frame(rstd_one, 0, 6)
    z_value = normed * g_one + b_one
    windows(win_one, jnp.where(inside, z_value * jax.nn.sigmoid(z_value), 0.0))
    hidden = conv(win_one, w1_ref, True, lags).astype(BF16)
    hid[2:6, 1:5] = hidden
    wide = hidden.astype(F32)
    put_stats(1, wide, wide * wide)
    send_stats(1)
    send_halo("hid")

    recv_stats(1)
    mean_two, rstd_two = moments(1)
    recv_halo("hid")
    recv_halo("err")
    normed = (hid[2:8].astype(F32) - per_frame(mean_two, 2, 8)) * per_frame(rstd_two, 2, 8)
    z_value = normed * g_two + b_two
    sig = jax.nn.sigmoid(z_value)
    slope = err[2:8] * sig * (1.0 + z_value * (1.0 - sig)) * g_two
    core_slope = jnp.where(in_pair, slope[0:4, 1:5], 0.0)
    put_stats(2, core_slope, core_slope * normed[0:4, 1:5])
    send_stats(2)

    past = (hid[0:2].astype(F32) - per_frame(mean_two, 0, 2)) * per_frame(rstd_two, 0, 2)
    past_z = past * g_two + b_two
    act = jnp.concatenate([past_z * jax.nn.sigmoid(past_z), z_value[0:4] * sig[0:4]], axis=0)
    windows(win_two, jnp.where(inside, act, 0.0))
    out_ref[...] = (conv(win_two, w2_ref, True, lags) + lat_ref[...].astype(F32)).astype(BF16)
    kernel_grad(win_two, cot_ref[...].astype(F32), lags, shared[0] if direct else g2_ref)
    if direct:
        scatter(0)

    recv_stats(2)
    p_two, q_two = totals(2)
    grad_hidden = per_frame(rstd_two, 2, 8) * (
        slope - per_frame(p_two, 2, 8) - normed * per_frame(q_two, 2, 8)
    )
    grad_hidden = jnp.where(inside, grad_hidden, 0.0).astype(BF16).astype(F32)
    kernel_grad(win_one, grad_hidden[0:4, 1:5], lags, shared[5] if direct else g1_ref)
    if direct:
        scatter(1)
    windows(win_back, grad_hidden)
    back_one = conv(win_back, w1t_ref, False, leads)

    normed = (lat_ref[...].astype(F32) - per_frame(mean_one, 2, 6)) * per_frame(rstd_one, 2, 6)
    z_value = normed * g_one + b_one
    sig = jax.nn.sigmoid(z_value)
    slope = back_one * sig * (1.0 + z_value * (1.0 - sig)) * g_one
    put_stats(3, slope, slope * normed)
    send_stats(3)
    if direct:
        gather(0)
        gather(1)
    recv_stats(3)
    p_one, q_one = totals(3)
    branch = per_frame(rstd_one, 2, 6) * (
        slope - per_frame(p_one, 2, 6) - normed * per_frame(q_one, 2, 6)
    )
    gl_ref[...] = (cot_ref[...].astype(F32) + branch).astype(BF16)

    if direct:
        finish(0, g2_ref)
        finish(1, g1_ref)
        settle(0)
        settle(1)
    for turn in range(4):
        for d, o in peers:
            guarded(within(d), lambda d=d, o=o: stat_copy(turn, d, o).wait_send())
    for name in halos:
        for item in halos[name]:
            guarded(within(spans[item[2]][0]), lambda item=item: halo_copy(*item).wait_send())


def banded(kernel, flip):
    if flip:
        kernel = jnp.swapaxes(kernel[:, ::-1, ::-1], 3, 4)
    taps = kernel.reshape(9, 3, kernel.shape[3], kernel.shape[4])
    none = jnp.zeros_like(taps[:, :1])
    left = jnp.concatenate([taps[:, 1:], none, taps[:, :1]], axis=1)
    right = jnp.concatenate([taps, none], axis=1)
    return jnp.concatenate([left, right], axis=3).reshape(9, 256, 128)


def unpacked(packed):
    packed = packed.reshape(9, 96, 128)
    later = packed[:, 0:64].reshape(9, 64, 2, 64).transpose(0, 2, 3, 1)
    early = packed[:, 64:96].reshape(9, 32, 2, 64).transpose(0, 3, 2, 1).reshape(9, 1, 64, 64)
    return jnp.concatenate([early, later], axis=1).reshape(3, 3, 3, 64, 64)


def per_device(
    n_tm, latents, cotangent, kernel_one, kernel_two, gain_one, offset_one, gain_two, offset_two,
    clip_id,
):
    n_frames, n_rows, flat = latents.shape
    channels = gain_one.shape[0]
    n_cols = flat // channels

    def shaped(field):
        field = field.reshape(n_frames, n_rows, n_cols // 2, 128)
        return jnp.pad(field, ((0, 0), (0, 0), (0, PAIRS - n_cols // 2), (0, 0)))

    ids = jnp.broadcast_to(jnp.pad((clip_id + 1).astype(F32), (0, 4))[:, None], (8, 128))
    vec = jnp.stack([gain_one, offset_one, gain_two, offset_two])
    vec = jnp.pad(jnp.concatenate([vec, vec], axis=1), ((0, 4), (0, 0)))
    block = jax.ShapeDtypeStruct((4, 4, PAIRS, 128), BF16)
    grads = jax.ShapeDtypeStruct((PIECES, 32, 128), F32)
    direct = 2 * n_tm == ALL
    sharing = [
        pltpu.VMEM((ALL, 32, 128), BF16),
        pltpu.VMEM((ALL, 32, 128), BF16),
        pltpu.VMEM((ALL, 32, 128), BF16),
        pltpu.SemaphoreType.DMA((2, ALL)),
        pltpu.SemaphoreType.DMA((2, ALL)),
    ]
    out, grad_latent, grad_one, grad_two = pl.pallas_call(
        functools.partial(kernel, n_tm, n_cols),
        out_shape=(block, block, grads, grads),
        in_specs=[pl.BlockSpec(memory_space=pltpu.VMEM)] * 8,
        out_specs=[pl.BlockSpec(memory_space=pltpu.VMEM)] * 4,
        scratch_shapes=[
            pltpu.VMEM((8, 6, PAIRS, 128), BF16),
            pltpu.VMEM((8, 6, PAIRS, 128), BF16),
            pltpu.VMEM((8, 6, PAIRS, 128), BF16),
            pltpu.VMEM((8, 6, PAIRS, 128), F32),
            pltpu.VMEM((4, SLOTS, 24, 128), F32),
            pltpu.VMEM((6, 6, PAIRS, 256), BF16),
            pltpu.VMEM((6, 6, PAIRS, 256), BF16),
            pltpu.VMEM((6, 6, PAIRS, 256), BF16),
            pltpu.VMEM((6, 6, PAIRS, 256), BF16),
            pltpu.SemaphoreType.DMA((4, SLOTS)),
            pltpu.SemaphoreType.DMA((4, SLOTS)),
            pltpu.SemaphoreType.DMA((14,)),
            pltpu.SemaphoreType.DMA((14,)),
        ]
        + (2 * sharing if direct else []),
        compiler_params=pltpu.CompilerParams(
            collective_id=0, has_side_effects=True, vmem_limit_bytes=48 * 1024 * 1024
        ),
    )(
        shaped(latents), shaped(cotangent), ids,
        banded(kernel_one, False), banded(kernel_one, True),
        banded(kernel_two, False), banded(kernel_two, True), vec,
    )
    if not direct:
        grad_one, grad_two = lax.psum((grad_one, grad_two), ("tm", "rows"))

    def plain(field):
        return field[:, :, : n_cols // 2].reshape(n_frames, n_rows, flat)

    return (plain(out), plain(grad_latent), unpacked(grad_one), unpacked(grad_two))


def solution(mesh):
    return jax.shard_map(
        functools.partial(per_device, mesh.shape["tm"]),
        mesh=mesh,
        in_specs=(
            P("tm", "rows", None), P("tm", "rows", None), P(), P(), P(), P(), P(), P(), P("tm"),
        ),
        out_specs=(P("tm", "rows", None), P("tm", "rows", None), P(), P()),
        check_vma=False,
    )
```

```python
import functools
import jax
import jax.numpy as jnp
from jax import lax
from jax.experimental import pallas as pl
from jax.experimental.pallas import tpu as pltpu
from jax.sharding import PartitionSpec as P

EPSILON = 1e-06
REACH = 4
SLOTS = 2 * (2 * REACH + 1)
OWN = 2 * REACH
PAIRS = 48
PIECES = 27
ALL = 32
MESH = pl.DeviceIdType.MESH
F32 = jnp.float32
BF16 = jnp.bfloat16


def kernel(
    n_tm, n_cols, lat_ref, cot_ref, ids_ref, k1_ref, k2_ref, vec_ref,
    out_ref, gl_ref, g1_ref, g2_ref,
    w1_ref, w1t_ref, w2_ref, w2t_ref, lat, cot, hid, err, stats, win_one, win_two, win_cot, win_back,
    stat_send, stat_recv, halo_send, halo_recv, *shared,
):
    direct = 2 * n_tm == ALL
    me = lax.axis_index("tm")
    core = lax.axis_index("rows")
    cells = 16 * PAIRS

    def within(d):
        if d == 0:
            return None
        return me + d < n_tm if d > 0 else me + d >= 0

    def guarded(cond, fn):
        if cond is None:
            fn()
        else:
            pl.when(cond)(fn)

    peers = [
        (d, o) for d in range(-REACH, REACH + 1) for o in range(2) if (d, o) != (0, 0)
    ]

    def device(d, o):
        return (me + d, core if o == 0 else 1 - core)

    def stat_copy(turn, d, o):
        slot = (REACH - d) * 2 + o
        return pltpu.make_async_remote_copy(
            src_ref=stats.at[turn, OWN],
            dst_ref=stats.at[turn, slot],
            send_sem=stat_send.at[turn, slot],
            recv_sem=stat_recv.at[turn, slot],
            device_id=device(d, o),
            device_id_type=MESH,
        )

    def send_stats(turn):
        for d, o in peers:
            guarded(within(d), lambda d=d, o=o: stat_copy(turn, d, o).start())

    def recv_stats(turn):
        for d, o in peers:
            guarded(within(-d), lambda d=d, o=o: stat_copy(turn, d, o).wait_recv())

    row_from = 4 - 3 * core
    row_to = 5 * core
    spans = {"past": (1, 4, 0, 2), "here": (0, 2, 2, 4), "next": (-1, 2, 6, 2)}

    def halo_copy(index, buf, kind, o):
        d, start, to, size = spans[kind]
        if o == 0:
            src = buf.at[pl.ds(start, size), pl.ds(1, 4)]
            dst = buf.at[pl.ds(to, size), pl.ds(1, 4)]
        else:
            src = buf.at[pl.ds(start, size), pl.ds(row_from, 1)]
            dst = buf.at[pl.ds(to, size), pl.ds(row_to, 1)]
        return pltpu.make_async_remote_copy(
            src_ref=src,
            dst_ref=dst,
            send_sem=halo_send.at[index],
            recv_sem=halo_recv.at[index],
            device_id=device(d, o),
            device_id_type=MESH,
        )

    halos = {
        "lat": [(0, lat, "past", 0), (1, lat, "past", 1), (2, lat, "here", 1)],
        "cot": [(3, cot, "next", 0), (4, cot, "next", 1), (5, cot, "here", 1)],
        "err": [(6, err, "next", 0), (7, err, "next", 1), (8, err, "here", 1)],
        "hid": [
            (9, hid, "past", 0), (10, hid, "past", 1), (11, hid, "here", 1),
            (12, hid, "next", 0), (13, hid, "next", 1),
        ],
    }

    def send_halo(name):
        for item in halos[name]:
            guarded(within(spans[item[2]][0]), lambda item=item: halo_copy(*item).start())

    def recv_halo(name):
        for item in halos[name]:
            guarded(
                within(-spans[item[2]][0]), lambda item=item: halo_copy(*item).wait_recv()
            )

    rank = 2 * me + core

    def around(step):
        target = (rank + step) % ALL
        return (target // 2, target % 2)

    def scatter_copy(which, step):
        parts, landing, sums, send, recv = shared[5 * which : 5 * which + 5]
        return pltpu.make_async_remote_copy(
            src_ref=parts.at[(rank + step) % ALL],
            dst_ref=landing.at[step],
            send_sem=send.at[0, step],
            recv_sem=recv.at[0, step],
            device_id=around(step),
            device_id_type=MESH,
        )

    def gather_copy(which, step):
        parts, landing, sums, send, recv = shared[5 * which : 5 * which + 5]
        return pltpu.make_async_remote_copy(
            src_ref=sums.at[rank],
            dst_ref=sums.at[rank],
            send_sem=send.at[1, step],
            recv_sem=recv.at[1, step],
            device_id=around(step),
            device_id_type=MESH,
        )

    owner = rank < PIECES

    def scatter(which):
        for step in range(1, ALL):
            pl.when((rank + step) % ALL < PIECES)(
                lambda step=step: scatter_copy(which, step).start()
            )

    def gather(which):
        parts, landing, sums, send, recv = shared[5 * which : 5 * which + 5]

        @pl.when(owner)
        def _():
            total = parts[rank].astype(F32)
            for step in range(1, ALL):
                scatter_copy(which, step).wait_recv()
            for step in range(1, ALL):
                total = total + landing[step].astype(F32)
            sums[rank] = total.astype(BF16)
            for step in range(1, ALL):
                gather_copy(which, step).start()

    def unpack(pieces, out):
        for index in range(9):
            rows = [pieces[3 * index + i].astype(F32) for i in range(3)]
            turned = jnp.concatenate(rows + [jnp.zeros((32, 128), F32)]).T
            early = turned[:, 64:96]
            out[3 * index] = jnp.concatenate([early[0:64], early[64:128]], axis=1)
            out[3 * index + 1] = turned[0:64, 0:64]
            out[3 * index + 2] = turned[64:128, 0:64]

    def band(source, ahead, back):
        none = jnp.zeros((64, 64), F32)
        for lag in range(3):
            for tap in range(3):
                first, second, third = (
                    source[9 * lag + 3 * tap + j].astype(F32) for j in range(3)
                )
                blocks = [
                    jnp.concatenate(two, axis=1).astype(BF16)
                    for two in (
                        (second, first), (third, second), (none, third), (first, none)
                    )
                ]
                index, mirror = 3 * lag + tap, 3 * lag + 2 - tap
                for i in range(4):
                    ahead[index, 64 * i : 64 * i + 64] = blocks[i]
                back[mirror, 0:64, 0:128] = blocks[0]
                back[mirror, 0:64, 128:256] = blocks[2]
                back[mirror, 64:128, 0:128] = blocks[1]
                back[mirror, 64:128, 128:256] = blocks[3]

    def finish(which, out):
        sums = shared[5 * which + 2]
        for step in range(1, ALL):
            pl.when((rank - step + ALL) % ALL < PIECES)(
                lambda step=step: gather_copy(which, step).wait_recv()
            )
        unpack(sums, out)

    def settle(which):
        for step in range(1, ALL):
            pl.when((rank + step) % ALL < PIECES)(
                lambda step=step: scatter_copy(which, step).wait_send()
            )
            pl.when(owner)(lambda step=step: gather_copy(which, step).wait_send())

    lane = lax.broadcasted_iota(jnp.int32, (1, 128), 1)
    low = lane < 64
    even = lane % 2 == 0

    def grouped(total):
        total = total + pltpu.roll(total, 64, 1)
        return total + jnp.where(even, pltpu.roll(total, 127, 1), pltpu.roll(total, 1, 1))

    def frame_sums(first, second):
        rows = [jnp.sum(v.reshape(4, 4 * PAIRS, 128), axis=1) for v in (first, second)]
        pad = jnp.zeros((4, 128), F32)
        return jnp.concatenate([rows[0], pad]), jnp.concatenate([rows[1], pad])

    def put_stats(turn, first, second):
        a, b = frame_sums(first, second)
        stats[turn, OWN, 0:8] = a
        stats[turn, OWN, 8:16] = b

    for buf in (lat, cot, hid, err):
        buf[...] = jnp.zeros_like(buf)
    stats[...] = jnp.zeros_like(stats)
    lat[2:6, 1:5] = lat_ref[...]
    cot[2:6, 1:5] = cot_ref[...]
    mine = lat_ref[...].astype(F32)
    put_stats(0, mine, mine * mine)
    stats[0, OWN, 16:24] = ids_ref[...]

    barrier = pltpu.get_barrier_semaphore()

    def greet(target):
        pl.semaphore_signal(barrier, inc=1, device_id=target, device_id_type=MESH)

    if direct:
        for step in range(1, ALL):
            greet(around(step))
        band(k1_ref, w1_ref, w1t_ref)
        pl.semaphore_wait(barrier, ALL - 1)
    else:
        for d, o in peers:
            guarded(within(d), lambda d=d, o=o: greet(device(d, o)))
        band(k1_ref, w1_ref, w1t_ref)
        reached = jnp.minimum(me, REACH) + jnp.minimum(n_tm - 1 - me, REACH)
        pl.semaphore_wait(barrier, 2 * reached + 1)

    send_stats(0)
    send_halo("lat")
    send_halo("cot")
    band(k2_ref, w2_ref, w2t_ref)

    g_one, b_one, g_two, b_two = (vec_ref[i : i + 1] for i in range(4))

    pair = lax.broadcasted_iota(jnp.int32, (6, PAIRS, 128), 1)
    image_row = lax.broadcasted_iota(jnp.int32, (6, PAIRS, 128), 0) + 4 * core
    inside = ((pair < n_cols // 2) & (image_row >= 1) & (image_row <= 8)).reshape(
        1, 6, PAIRS, 128
    )
    in_pair = lax.broadcasted_iota(jnp.int32, (1, 1, PAIRS, 128), 2) < n_cols // 2

    def windows(win, field):
        rows = 36 * PAIRS
        cur = field.reshape(rows, 128)
        side = jnp.where(low, pltpu.roll(cur, rows - 1, 0), pltpu.roll(cur, 1, 0))
        win[:, :, :, 0:128] = cur.reshape(6, 6, PAIRS, 128).astype(BF16)
        win[:, :, :, 128:256] = side.reshape(6, 6, PAIRS, 128).astype(BF16)

    def conv(win, weight, first, masks):
        total = None
        for lag in range(3):
            frame = 2 - lag if first else lag
            part = None
            for tap in range(3):
                patch = win[frame : frame + 4, tap : tap + 4].reshape(cells, 256)
                term = lax.dot_general(
                    patch,
                    weight[3 * lag + tap],
                    (((1,), (0 if first else 1,)), ((), ())),
                    preferred_element_type=F32,
                )
                part = term if part is None else part + term
            part = part.reshape(4, 4, PAIRS, 128)
            if lag > 0:
                part = jnp.where(masks[lag], part, 0.0)
            total = part if total is None else total + part
        return jnp.where(in_pair, total, 0.0)

    def kernel_grad(win, grad, masks, out):
        for lag in range(3):
            kept = grad if lag == 0 else jnp.where(masks[lag], grad, 0.0)
            turned = kept.reshape(cells, 128).T.astype(BF16)
            for tap in range(3):
                patch = win[2 - lag : 6 - lag, tap : tap + 4].reshape(cells, 256)
                prod = jnp.dot(turned, patch, preferred_element_type=F32)
                a_lo, a_hi = prod[0:64, 0:128], prod[0:64, 128:256]
                b_lo, b_hi = prod[64:128, 0:128], prod[64:128, 128:256]
                later = a_lo + pltpu.roll(jnp.where(low, b_hi, b_lo), 64, 1)
                early = a_hi + pltpu.roll(b_lo, 64, 1)
                packed = jnp.where(low, pltpu.roll(early[0:32], 64, 1), early[32:64])
                index = 3 * (3 * lag + tap)
                out[index] = later[0:32].astype(out.dtype)
                out[index + 1] = later[32:64].astype(out.dtype)
                out[index + 2] = packed.astype(out.dtype)

    recv_stats(0)
    all_ids = stats[0, :, 16:24].reshape(SLOTS * 8, 128)
    before, own_ids, after = (
        stats[0, OWN - 2, 16:24], stats[0, OWN, 16:24], stats[0, OWN + 2, 16:24]
    )
    ids = [before[2:3], before[3:4]] + [own_ids[f : f + 1] for f in range(4)]
    ids = ids + [after[0:1], after[1:2]]
    match = [(all_ids == i).astype(F32) for i in ids]
    per_slot = float(4 * n_cols * 2)
    count = jnp.concatenate([jnp.sum(m, axis=0, keepdims=True) for m in match])
    count = jnp.maximum(count, 1.0) * per_slot

    def totals(turn):
        both = []
        for part in range(2):
            table = stats[turn, :, 8 * part : 8 * part + 8].reshape(SLOTS * 8, 128)
            rows = [jnp.sum(m * table, axis=0, keepdims=True) for m in match]
            both.append(grouped(jnp.concatenate(rows)) / count)
        return both

    def per_frame(rows, lo, hi):
        return rows[lo:hi].reshape(hi - lo, 1, 1, 128)

    def same(lag, direction):
        rows = [
            jnp.broadcast_to(
                (ids[2 + f] == ids[2 + f + direction * lag]).astype(F32).reshape(1, 1, 1, 128),
                (1, 1, 1, 128),
            )
            for f in range(4)
        ]
        return jnp.concatenate(rows, axis=0) > 0.5

    lags = [None, same(1, -1), same(2, -1)]
    leads = [None, same(1, 1), same(2, 1)]

    def moments(turn):
        mean, square = totals(turn)
        return mean, lax.rsqrt(jnp.maximum(square - mean * mean, 0.0) + EPSILON)

    mean_one, rstd_one = moments(0)
    recv_halo("lat")
    normed = (lat[0:6].astype(F32) - per_frame(mean_one, 0, 6)) * per_frame(rstd_one, 0, 6)
    z_value = normed * g_one + b_one
    windows(win_one, jnp.where(inside, z_value * jax.nn.sigmoid(z_value), 0.0))
    hidden = conv(win_one, w1_ref, True, lags).astype(BF16)
    hid[2:6, 1:5] = hidden
    wide = hidden.astype(F32)
    put_stats(1, wide, wide * wide)
    send_stats(1)
    send_halo("hid")

    recv_halo("cot")
    windows(win_cot, cot[2:8].astype(F32))
    back_two = conv(win_cot, w2t_ref, False, leads)
    err[2:6, 1:5] = back_two
    send_halo("err")

    recv_stats(1)
    mean_two, rstd_two = moments(1)
    recv_halo("hid")
    normed = (hid[...].astype(F32) - per_frame(mean_two, 0, 8)) * per_frame(rstd_two, 0, 8)
    z_value = normed * g_two + b_two
    sig = jax.nn.sigmoid(z_value)
    windows(win_two, jnp.where(inside, z_value[0:6] * sig[0:6], 0.0))
    out_ref[...] = (conv(win_two, w2_ref, True, lags) + lat_ref[...].astype(F32)).astype(BF16)
    recv_halo("err")
    normed, z_value, sig = normed[2:8], z_value[2:8], sig[2:8]
    slope = err[2:8] * sig * (1.0 + z_value * (1.0 - sig)) * g_two
    core_slope = jnp.where(in_pair, slope[0:4, 1:5], 0.0)
    put_stats(2, core_slope, core_slope * normed[0:4, 1:5])
    send_stats(2)
    kernel_grad(win_two, cot_ref[...].astype(F32), lags, shared[0])
    if direct:
        scatter(0)

    recv_stats(2)
    p_two, q_two = totals(2)
    grad_hidden = per_frame(rstd_two, 2, 8) * (
        slope - per_frame(p_two, 2, 8) - normed * per_frame(q_two, 2, 8)
    )
    grad_hidden = jnp.where(inside, grad_hidden, 0.0).astype(BF16).astype(F32)
    kernel_grad(win_one, grad_hidden[0:4, 1:5], lags, shared[5 if direct else 1])
    if direct:
        scatter(1)
        gather(0)
    windows(win_back, grad_hidden)
    back_one = conv(win_back, w1t_ref, False, leads)

    normed = (lat_ref[...].astype(F32) - per_frame(mean_one, 2, 6)) * per_frame(rstd_one, 2, 6)
    z_value = normed * g_one + b_one
    sig = jax.nn.sigmoid(z_value)
    slope = back_one * sig * (1.0 + z_value * (1.0 - sig)) * g_one
    put_stats(3, slope, slope * normed)
    send_stats(3)
    if direct:
        gather(1)
        finish(0, g2_ref)
    recv_stats(3)
    p_one, q_one = totals(3)
    branch = per_frame(rstd_one, 2, 6) * (
        slope - per_frame(p_one, 2, 6) - normed * per_frame(q_one, 2, 6)
    )
    gl_ref[...] = (cot_ref[...].astype(F32) + branch).astype(BF16)

    if direct:
        finish(1, g1_ref)
        settle(0)
        settle(1)
    else:
        unpack(shared[0], g2_ref)
        unpack(shared[1], g1_ref)
    for turn in range(4):
        for d, o in peers:
            guarded(within(d), lambda d=d, o=o: stat_copy(turn, d, o).wait_send())
    for name in halos:
        for item in halos[name]:
            guarded(within(spans[item[2]][0]), lambda item=item: halo_copy(*item).wait_send())


def per_device(
    n_tm, latents, cotangent, kernel_one, kernel_two, gain_one, offset_one, gain_two, offset_two,
    clip_id,
):
    n_frames, n_rows, flat = latents.shape
    channels = gain_one.shape[0]
    n_cols = flat // channels

    def shaped(field):
        field = field.reshape(n_frames, n_rows, n_cols // 2, 128)
        return jnp.pad(field, ((0, 0), (0, 0), (0, PAIRS - n_cols // 2), (0, 0)))

    ids = jnp.broadcast_to(jnp.pad((clip_id + 1).astype(F32), (0, 4))[:, None], (8, 128))
    vec = jnp.stack([gain_one, offset_one, gain_two, offset_two])
    vec = jnp.pad(jnp.concatenate([vec, vec], axis=1), ((0, 4), (0, 0)))
    block = jax.ShapeDtypeStruct((4, 4, PAIRS, 128), BF16)
    grads = jax.ShapeDtypeStruct((27, 64, 64), F32)
    direct = 2 * n_tm == ALL
    sharing = [
        pltpu.VMEM((ALL, 32, 128), BF16),
        pltpu.VMEM((ALL, 32, 128), BF16),
        pltpu.VMEM((ALL, 32, 128), BF16),
        pltpu.SemaphoreType.DMA((2, ALL)),
        pltpu.SemaphoreType.DMA((2, ALL)),
    ]
    out, grad_latent, grad_one, grad_two = pl.pallas_call(
        functools.partial(kernel, n_tm, n_cols),
        out_shape=(block, block, grads, grads),
        in_specs=[pl.BlockSpec(memory_space=pltpu.VMEM)] * 6,
        out_specs=[pl.BlockSpec(memory_space=pltpu.VMEM)] * 4,
        scratch_shapes=[
            pltpu.VMEM((9, 256, 128), BF16),
            pltpu.VMEM((9, 128, 256), BF16),
            pltpu.VMEM((9, 256, 128), BF16),
            pltpu.VMEM((9, 128, 256), BF16),
            pltpu.VMEM((8, 6, PAIRS, 128), BF16),
            pltpu.VMEM((8, 6, PAIRS, 128), BF16),
            pltpu.VMEM((8, 6, PAIRS, 128), BF16),
            pltpu.VMEM((8, 6, PAIRS, 128), F32),
            pltpu.VMEM((4, SLOTS, 24, 128), F32),
            pltpu.VMEM((6, 6, PAIRS, 256), BF16),
            pltpu.VMEM((6, 6, PAIRS, 256), BF16),
            pltpu.VMEM((6, 6, PAIRS, 256), BF16),
            pltpu.VMEM((6, 6, PAIRS, 256), BF16),
            pltpu.SemaphoreType.DMA((4, SLOTS)),
            pltpu.SemaphoreType.DMA((4, SLOTS)),
            pltpu.SemaphoreType.DMA((14,)),
            pltpu.SemaphoreType.DMA((14,)),
        ]
        + (2 * sharing if direct else [pltpu.VMEM((PIECES, 32, 128), F32)] * 2),
        compiler_params=pltpu.CompilerParams(
            collective_id=0, has_side_effects=True, vmem_limit_bytes=48 * 1024 * 1024
        ),
    )(
        shaped(latents), shaped(cotangent), ids,
        kernel_one.reshape(27, 64, 64), kernel_two.reshape(27, 64, 64), vec,
    )
    if not direct:
        grad_one, grad_two = lax.psum((grad_one, grad_two), ("tm", "rows"))

    def plain(field):
        return field[:, :, : n_cols // 2].reshape(n_frames, n_rows, flat)

    shape = kernel_one.shape
    return (plain(out), plain(grad_latent), grad_one.reshape(shape), grad_two.reshape(shape))


def solution(mesh):
    return jax.shard_map(
        functools.partial(per_device, mesh.shape["tm"]),
        mesh=mesh,
        in_specs=(
            P("tm", "rows", None), P("tm", "rows", None), P(), P(), P(), P(), P(), P(), P("tm"),
        ),
        out_specs=(P("tm", "rows", None), P("tm", "rows", None), P(), P()),
        check_vma=False,
    )
```

```python
import functools
import jax
import jax.numpy as jnp
from jax import lax
from jax.experimental import pallas as pl
from jax.experimental.pallas import tpu as pltpu
from jax.sharding import PartitionSpec as P

EPSILON = 1e-06
REACH = 4
SLOTS = 2 * (2 * REACH + 1)
OWN = 2 * REACH
PAIRS = 48
PIECES = 27
ALL = 32
MESH = pl.DeviceIdType.MESH
F32 = jnp.float32
BF16 = jnp.bfloat16


def kernel(
    n_tm, n_cols, lat_ref, cot_ref, ids_ref, k1_ref, k2_ref, vec_ref,
    out_ref, gl_ref, g1_ref, g2_ref,
    w1_ref, w1t_ref, w2_ref, w2t_ref, lat, cot, hid, err, stats, win_one, win_two, win_cot, win_back,
    stat_send, stat_recv, halo_send, halo_recv, *shared,
):
    direct = 2 * n_tm == ALL
    me = lax.axis_index("tm")
    core = lax.axis_index("rows")
    cells = 16 * PAIRS

    def within(d):
        if d == 0:
            return None
        return me + d < n_tm if d > 0 else me + d >= 0

    def guarded(cond, fn):
        if cond is None:
            fn()
        else:
            pl.when(cond)(fn)

    peers = [
        (d, o) for d in range(-REACH, REACH + 1) for o in range(2) if (d, o) != (0, 0)
    ]

    def device(d, o):
        return (me + d, core if o == 0 else 1 - core)

    def stat_copy(turn, d, o):
        slot = (REACH - d) * 2 + o
        return pltpu.make_async_remote_copy(
            src_ref=stats.at[turn, OWN],
            dst_ref=stats.at[turn, slot],
            send_sem=stat_send.at[turn, slot],
            recv_sem=stat_recv.at[turn, slot],
            device_id=device(d, o),
            device_id_type=MESH,
        )

    def send_stats(turn):
        for d, o in peers:
            guarded(within(d), lambda d=d, o=o: stat_copy(turn, d, o).start())

    def recv_stats(turn):
        for d, o in peers:
            guarded(within(-d), lambda d=d, o=o: stat_copy(turn, d, o).wait_recv())

    row_from = 4 - 3 * core
    row_to = 5 * core
    spans = {"past": (1, 4, 0, 2), "here": (0, 2, 2, 4), "next": (-1, 2, 6, 2)}

    def halo_copy(index, buf, kind, o):
        d, start, to, size = spans[kind]
        if o == 0:
            src = buf.at[pl.ds(start, size), pl.ds(1, 4)]
            dst = buf.at[pl.ds(to, size), pl.ds(1, 4)]
        else:
            src = buf.at[pl.ds(start, size), pl.ds(row_from, 1)]
            dst = buf.at[pl.ds(to, size), pl.ds(row_to, 1)]
        return pltpu.make_async_remote_copy(
            src_ref=src,
            dst_ref=dst,
            send_sem=halo_send.at[index],
            recv_sem=halo_recv.at[index],
            device_id=device(d, o),
            device_id_type=MESH,
        )

    halos = {
        "lat": [(0, lat, "past", 0), (1, lat, "past", 1), (2, lat, "here", 1)],
        "cot": [(3, cot, "next", 0), (4, cot, "next", 1), (5, cot, "here", 1)],
        "err": [(6, err, "next", 0), (7, err, "next", 1), (8, err, "here", 1)],
        "hid": [
            (9, hid, "past", 0), (10, hid, "past", 1), (11, hid, "here", 1),
            (12, hid, "next", 0), (13, hid, "next", 1),
        ],
    }

    def send_halo(name):
        for item in halos[name]:
            guarded(within(spans[item[2]][0]), lambda item=item: halo_copy(*item).start())

    def recv_halo(name):
        for item in halos[name]:
            guarded(
                within(-spans[item[2]][0]), lambda item=item: halo_copy(*item).wait_recv()
            )

    rank = 2 * me + core

    def around(step):
        target = (rank + step) % ALL
        return (target // 2, target % 2)

    def scatter_copy(which, step):
        parts, landing, sums, send, recv = shared[5 * which : 5 * which + 5]
        return pltpu.make_async_remote_copy(
            src_ref=parts.at[(rank + step) % ALL],
            dst_ref=landing.at[step],
            send_sem=send.at[0, step],
            recv_sem=recv.at[0, step],
            device_id=around(step),
            device_id_type=MESH,
        )

    def gather_copy(which, step):
        parts, landing, sums, send, recv = shared[5 * which : 5 * which + 5]
        return pltpu.make_async_remote_copy(
            src_ref=sums.at[rank],
            dst_ref=sums.at[rank],
            send_sem=send.at[1, step],
            recv_sem=recv.at[1, step],
            device_id=around(step),
            device_id_type=MESH,
        )

    owner = rank < PIECES

    def scatter(which):
        for step in range(1, ALL):
            pl.when((rank + step) % ALL < PIECES)(
                lambda step=step: scatter_copy(which, step).start()
            )

    def gather(which):
        parts, landing, sums, send, recv = shared[5 * which : 5 * which + 5]

        @pl.when(owner)
        def _():
            total = parts[rank].astype(F32)
            for step in range(1, ALL):
                scatter_copy(which, step).wait_recv()
            for step in range(1, ALL):
                total = total + landing[step].astype(F32)
            sums[rank] = total.astype(BF16)
            for step in range(1, ALL):
                gather_copy(which, step).start()

    def unpack(pieces, out):
        for index in range(9):
            rows = [pieces[3 * index + i].astype(F32) for i in range(3)]
            turned = jnp.concatenate(rows + [jnp.zeros((32, 128), F32)]).T
            early = turned[:, 64:96]
            out[3 * index] = jnp.concatenate([early[0:64], early[64:128]], axis=1)
            out[3 * index + 1] = turned[0:64, 0:64]
            out[3 * index + 2] = turned[64:128, 0:64]

    def band(source, ahead, back):
        none = jnp.zeros((64, 64), F32)
        for lag in range(3):
            for tap in range(3):
                first, second, third = (
                    source[9 * lag + 3 * tap + j].astype(F32) for j in range(3)
                )
                blocks = [
                    jnp.concatenate(two, axis=1).astype(BF16)
                    for two in (
                        (second, first), (third, second), (none, third), (first, none)
                    )
                ]
                index, mirror = 3 * lag + tap, 3 * lag + 2 - tap
                for i in range(4):
                    ahead[index, 64 * i : 64 * i + 64] = blocks[i]
                back[mirror, 0:64, 0:128] = blocks[0]
                back[mirror, 0:64, 128:256] = blocks[2]
                back[mirror, 64:128, 0:128] = blocks[1]
                back[mirror, 64:128, 128:256] = blocks[3]

    def finish(which, out):
        sums = shared[5 * which + 2]
        for step in range(1, ALL):
            pl.when((rank - step + ALL) % ALL < PIECES)(
                lambda step=step: gather_copy(which, step).wait_recv()
            )
        unpack(sums, out)

    def settle(which):
        for step in range(1, ALL):
            pl.when((rank + step) % ALL < PIECES)(
                lambda step=step: scatter_copy(which, step).wait_send()
            )
            pl.when(owner)(lambda step=step: gather_copy(which, step).wait_send())

    lane = lax.broadcasted_iota(jnp.int32, (1, 128), 1)
    low = lane < 64
    even = lane % 2 == 0

    def grouped(total):
        total = total + pltpu.roll(total, 64, 1)
        return total + jnp.where(even, pltpu.roll(total, 127, 1), pltpu.roll(total, 1, 1))

    def frame_sums(first, second):
        rows = [jnp.sum(v.reshape(4, 4 * PAIRS, 128), axis=1) for v in (first, second)]
        pad = jnp.zeros((4, 128), F32)
        return jnp.concatenate([rows[0], pad]), jnp.concatenate([rows[1], pad])

    def put_stats(turn, first, second):
        a, b = frame_sums(first, second)
        stats[turn, OWN, 0:8] = a
        stats[turn, OWN, 8:16] = b

    for buf in (lat, cot, hid, err):
        buf[...] = jnp.zeros_like(buf)
    stats[...] = jnp.zeros_like(stats)
    lat[2:6, 1:5] = lat_ref[...]
    cot[2:6, 1:5] = cot_ref[...]
    mine = lat_ref[...].astype(F32)
    put_stats(0, mine, mine * mine)
    stats[0, OWN, 16:24] = ids_ref[...]

    barrier = pltpu.get_barrier_semaphore()

    def greet(target):
        pl.semaphore_signal(barrier, inc=1, device_id=target, device_id_type=MESH)

    if direct:
        for step in range(1, ALL):
            greet(around(step))
        band(k1_ref, w1_ref, w1t_ref)
        pl.semaphore_wait(barrier, ALL - 1)
    else:
        for d, o in peers:
            guarded(within(d), lambda d=d, o=o: greet(device(d, o)))
        band(k1_ref, w1_ref, w1t_ref)
        reached = jnp.minimum(me, REACH) + jnp.minimum(n_tm - 1 - me, REACH)
        pl.semaphore_wait(barrier, 2 * reached + 1)

    send_stats(0)
    send_halo("lat")
    send_halo("cot")
    band(k2_ref, w2_ref, w2t_ref)

    g_one, b_one, g_two, b_two = (vec_ref[i : i + 1] for i in range(4))

    pair = lax.broadcasted_iota(jnp.int32, (6, PAIRS, 128), 1)
    image_row = lax.broadcasted_iota(jnp.int32, (6, PAIRS, 128), 0) + 4 * core
    inside = ((pair < n_cols // 2) & (image_row >= 1) & (image_row <= 8)).reshape(
        1, 6, PAIRS, 128
    )
    in_pair = lax.broadcasted_iota(jnp.int32, (1, 1, PAIRS, 128), 2) < n_cols // 2

    def windows(win, field):
        rows = 36 * PAIRS
        cur = field.reshape(rows, 128)
        side = jnp.where(low, pltpu.roll(cur, rows - 1, 0), pltpu.roll(cur, 1, 0))
        win[:, :, :, 0:128] = cur.reshape(6, 6, PAIRS, 128).astype(BF16)
        win[:, :, :, 128:256] = side.reshape(6, 6, PAIRS, 128).astype(BF16)

    def conv(win, weight, first, masks):
        total = None
        for lag in range(3):
            frame = 2 - lag if first else lag
            part = None
            for tap in range(3):
                patch = win[frame : frame + 4, tap : tap + 4].reshape(cells, 256)
                term = lax.dot_general(
                    patch,
                    weight[3 * lag + tap],
                    (((1,), (0 if first else 1,)), ((), ())),
                    preferred_element_type=F32,
                )
                part = term if part is None else part + term
            part = part.reshape(4, 4, PAIRS, 128)
            if lag > 0:
                part = jnp.where(masks[lag], part, 0.0)
            total = part if total is None else total + part
        return jnp.where(in_pair, total, 0.0)

    def kernel_grad(win, grad, masks, out):
        for lag in range(3):
            kept = grad if lag == 0 else jnp.where(masks[lag], grad, 0.0)
            turned = kept.reshape(cells, 128).astype(BF16).T
            for tap in range(3):
                patch = win[2 - lag : 6 - lag, tap : tap + 4].reshape(cells, 256)
                prod = jnp.dot(turned, patch, preferred_element_type=F32)
                a_lo, a_hi = prod[0:64, 0:128], prod[0:64, 128:256]
                b_lo, b_hi = prod[64:128, 0:128], prod[64:128, 128:256]
                later = a_lo + pltpu.roll(jnp.where(low, b_hi, b_lo), 64, 1)
                early = a_hi + pltpu.roll(b_lo, 64, 1)
                packed = jnp.where(low, pltpu.roll(early[0:32], 64, 1), early[32:64])
                index = 3 * (3 * lag + tap)
                out[index] = later[0:32].astype(out.dtype)
                out[index + 1] = later[32:64].astype(out.dtype)
                out[index + 2] = packed.astype(out.dtype)

    recv_stats(0)
    all_ids = stats[0, :, 16:24].reshape(SLOTS * 8, 128)
    before, own_ids, after = (
        stats[0, OWN - 2, 16:24], stats[0, OWN, 16:24], stats[0, OWN + 2, 16:24]
    )
    ids = [before[2:3], before[3:4]] + [own_ids[f : f + 1] for f in range(4)]
    ids = ids + [after[0:1], after[1:2]]
    match = [(all_ids == i).astype(F32) for i in ids]
    per_slot = float(4 * n_cols * 2)
    count = jnp.concatenate([jnp.sum(m, axis=0, keepdims=True) for m in match])
    count = jnp.maximum(count, 1.0) * per_slot

    def totals(turn):
        both = []
        for part in range(2):
            table = stats[turn, :, 8 * part : 8 * part + 8].reshape(SLOTS * 8, 128)
            rows = [jnp.sum(m * table, axis=0, keepdims=True) for m in match]
            both.append(grouped(jnp.concatenate(rows)) / count)
        return both

    def per_frame(rows, lo, hi):
        return rows[lo:hi].reshape(hi - lo, 1, 1, 128)

    def same(lag, direction):
        rows = [
            jnp.broadcast_to(
                (ids[2 + f] == ids[2 + f + direction * lag]).astype(F32).reshape(1, 1, 1, 128),
                (1, 1, 1, 128),
            )
            for f in range(4)
        ]
        return jnp.concatenate(rows, axis=0) > 0.5

    lags = [None, same(1, -1), same(2, -1)]
    leads = [None, same(1, 1), same(2, 1)]

    def moments(turn):
        mean, square = totals(turn)
        return mean, lax.rsqrt(jnp.maximum(square - mean * mean, 0.0) + EPSILON)

    mean_one, rstd_one = moments(0)
    recv_halo("lat")
    normed = (lat[0:6].astype(F32) - per_frame(mean_one, 0, 6)) * per_frame(rstd_one, 0, 6)
    z_value = normed * g_one + b_one
    windows(win_one, jnp.where(inside, z_value * jax.nn.sigmoid(z_value), 0.0))
    hidden = conv(win_one, w1_ref, True, lags).astype(BF16)
    hid[2:6, 1:5] = hidden
    wide = hidden.astype(F32)
    put_stats(1, wide, wide * wide)
    send_stats(1)
    send_halo("hid")

    recv_halo("cot")
    windows(win_cot, cot[2:8].astype(F32))
    back_two = conv(win_cot, w2t_ref, False, leads)
    err[2:6, 1:5] = back_two
    send_halo("err")

    recv_stats(1)
    mean_two, rstd_two = moments(1)
    recv_halo("hid")
    normed = (hid[...].astype(F32) - per_frame(mean_two, 0, 8)) * per_frame(rstd_two, 0, 8)
    z_value = normed * g_two + b_two
    sig = jax.nn.sigmoid(z_value)
    windows(win_two, jnp.where(inside, z_value[0:6] * sig[0:6], 0.0))
    out_ref[...] = (conv(win_two, w2_ref, True, lags) + lat_ref[...].astype(F32)).astype(BF16)
    recv_halo("err")
    normed, z_value, sig = normed[2:8], z_value[2:8], sig[2:8]
    slope = err[2:8] * sig * (1.0 + z_value * (1.0 - sig)) * g_two
    core_slope = jnp.where(in_pair, slope[0:4, 1:5], 0.0)
    put_stats(2, core_slope, core_slope * normed[0:4, 1:5])
    send_stats(2)
    kernel_grad(win_two, cot_ref[...].astype(F32), lags, shared[0])
    if direct:
        scatter(0)

    recv_stats(2)
    p_two, q_two = totals(2)
    grad_hidden = per_frame(rstd_two, 2, 8) * (
        slope - per_frame(p_two, 2, 8) - normed * per_frame(q_two, 2, 8)
    )
    grad_hidden = jnp.where(inside, grad_hidden, 0.0).astype(BF16).astype(F32)
    kernel_grad(win_one, grad_hidden[0:4, 1:5], lags, shared[5 if direct else 1])
    if direct:
        scatter(1)
        gather(0)
    windows(win_back, grad_hidden)
    back_one = conv(win_back, w1t_ref, False, leads)

    normed = (lat_ref[...].astype(F32) - per_frame(mean_one, 2, 6)) * per_frame(rstd_one, 2, 6)
    z_value = normed * g_one + b_one
    sig = jax.nn.sigmoid(z_value)
    slope = back_one * sig * (1.0 + z_value * (1.0 - sig)) * g_one
    put_stats(3, slope, slope * normed)
    send_stats(3)
    if direct:
        gather(1)
        finish(0, g2_ref)
    recv_stats(3)
    p_one, q_one = totals(3)
    branch = per_frame(rstd_one, 2, 6) * (
        slope - per_frame(p_one, 2, 6) - normed * per_frame(q_one, 2, 6)
    )
    gl_ref[...] = (cot_ref[...].astype(F32) + branch).astype(BF16)

    if direct:
        settle(0)
    else:
        unpack(shared[0], g2_ref)
        unpack(shared[1], g1_ref)
    for turn in range(4):
        for d, o in peers:
            guarded(within(d), lambda d=d, o=o: stat_copy(turn, d, o).wait_send())
    for name in halos:
        for item in halos[name]:
            guarded(within(spans[item[2]][0]), lambda item=item: halo_copy(*item).wait_send())
    if direct:
        finish(1, g1_ref)
        settle(1)


def per_device(
    n_tm, latents, cotangent, kernel_one, kernel_two, gain_one, offset_one, gain_two, offset_two,
    clip_id,
):
    n_frames, n_rows, flat = latents.shape
    channels = gain_one.shape[0]
    n_cols = flat // channels

    def shaped(field):
        field = field.reshape(n_frames, n_rows, n_cols // 2, 128)
        return jnp.pad(field, ((0, 0), (0, 0), (0, PAIRS - n_cols // 2), (0, 0)))

    ids = jnp.broadcast_to(jnp.pad((clip_id + 1).astype(F32), (0, 4))[:, None], (8, 128))
    vec = jnp.stack([gain_one, offset_one, gain_two, offset_two])
    vec = jnp.pad(jnp.concatenate([vec, vec], axis=1), ((0, 4), (0, 0)))
    block = jax.ShapeDtypeStruct((4, 4, PAIRS, 128), BF16)
    grads = jax.ShapeDtypeStruct((27, 64, 64), F32)
    direct = 2 * n_tm == ALL
    sharing = [
        pltpu.VMEM((ALL, 32, 128), BF16),
        pltpu.VMEM((ALL, 32, 128), BF16),
        pltpu.VMEM((ALL, 32, 128), BF16),
        pltpu.SemaphoreType.DMA((2, ALL)),
        pltpu.SemaphoreType.DMA((2, ALL)),
    ]
    out, grad_latent, grad_one, grad_two = pl.pallas_call(
        functools.partial(kernel, n_tm, n_cols),
        out_shape=(block, block, grads, grads),
        in_specs=[pl.BlockSpec(memory_space=pltpu.VMEM)] * 6,
        out_specs=[pl.BlockSpec(memory_space=pltpu.VMEM)] * 4,
        scratch_shapes=[
            pltpu.VMEM((9, 256, 128), BF16),
            pltpu.VMEM((9, 128, 256), BF16),
            pltpu.VMEM((9, 256, 128), BF16),
            pltpu.VMEM((9, 128, 256), BF16),
            pltpu.VMEM((8, 6, PAIRS, 128), BF16),
            pltpu.VMEM((8, 6, PAIRS, 128), BF16),
            pltpu.VMEM((8, 6, PAIRS, 128), BF16),
            pltpu.VMEM((8, 6, PAIRS, 128), F32),
            pltpu.VMEM((4, SLOTS, 24, 128), F32),
            pltpu.VMEM((6, 6, PAIRS, 256), BF16),
            pltpu.VMEM((6, 6, PAIRS, 256), BF16),
            pltpu.VMEM((6, 6, PAIRS, 256), BF16),
            pltpu.VMEM((6, 6, PAIRS, 256), BF16),
            pltpu.SemaphoreType.DMA((4, SLOTS)),
            pltpu.SemaphoreType.DMA((4, SLOTS)),
            pltpu.SemaphoreType.DMA((14,)),
            pltpu.SemaphoreType.DMA((14,)),
        ]
        + (2 * sharing if direct else [pltpu.VMEM((PIECES, 32, 128), F32)] * 2),
        compiler_params=pltpu.CompilerParams(
            collective_id=0, has_side_effects=True, vmem_limit_bytes=48 * 1024 * 1024
        ),
    )(
        shaped(latents), shaped(cotangent), ids,
        kernel_one.reshape(27, 64, 64), kernel_two.reshape(27, 64, 64), vec,
    )
    if not direct:
        grad_one, grad_two = lax.psum((grad_one, grad_two), ("tm", "rows"))

    def plain(field):
        return field[:, :, : n_cols // 2].reshape(n_frames, n_rows, flat)

    shape = kernel_one.shape
    return (plain(out), plain(grad_latent), grad_one.reshape(shape), grad_two.reshape(shape))


def solution(mesh):
    return jax.shard_map(
        functools.partial(per_device, mesh.shape["tm"]),
        mesh=mesh,
        in_specs=(
            P("tm", "rows", None), P("tm", "rows", None), P(), P(), P(), P(), P(), P(), P("tm"),
        ),
        out_specs=(P("tm", "rows", None), P("tm", "rows", None), P(), P()),
        check_vma=False,
    )
```
